1024 devices in a mesh: seq: 64 (over y_hi, z), row: 2 (over core), col: 8 (over x, y_lo).
Axes of the slice: x: 4, y: 8 (y_hi: 4, y_lo: 2; y = y_hi * 2 + y_lo), z: 16, core: 2. Of those that a mesh axis runs over, the one named last changes fastest.
Arguments:
- tokens: bfloat16 [8192, 4096], P('seq', 'row'), may hold values from -40 to 40
- block_order: int32 [128], replicated, may hold values from 0 to 127, as said below
- query_weight: bfloat16 [4096, 4096], P('row', 'col'), may hold values from -0.09375 to 0.09375
- key_weight: bfloat16 [4096, 1024], P('row', 'col'), may hold values from -0.09375 to 0.09375
- value_weight: bfloat16 [4096, 1024], P('row', 'col'), may hold values from -0.09375 to 0.09375
- output_weight: bfloat16 [4096, 4096], P('col'), may hold values from -0.09375 to 0.09375
Outputs:
- layer_out: float32 [8192, 4096], P('seq', ('row', 'col'))
The draws below stay inside these ranges and needn't reach their ends.
Inputs may be any that keep to these rules, and one draw needn't show every extreme that they name: Slots 2 d and 2 d + 1 are the rows of device d along seq; for every d, block_order[2 d + 1] = 127 - block_order[2 d] with block_order[2 d] < 64, and every half-block appears once.
All inputs are finite; a program needn't handle non-finite values.
Results may differ from the reference program's by a relative error of at most 0.012.
The reference program's roundings to bfloat16 on the way (of `attended`) count: a program that leaves them out, or rounds other values in their place, can miss the bound.
Values may be sent and summed in bfloat16 or wider, within the bound.
No kernel may reach another device: no remote copies, remote signals or barrier semaphores. Data moves between devices by JAX's collectives and lax.ppermute only.
A program may use at most 32 MiB of HBM per device.

```python
import jax
import jax.numpy as jnp
from jax import lax

D = 4096
H = 32
KV = 8
HD = 128
TOK_DEV = 128
TOKENS = 8192
N_SEQ = 64


def draw_tokens(key, part):
    first_key = jax.random.fold_in(key, 0)
    base = jax.random.normal(first_key, (TOKENS, D), jnp.float32)
    values = base
    return jnp.clip(values, -40.0, 40.0).astype(jnp.bfloat16)


def draw_block_order(key, part):
    lower = jax.random.permutation(key, N_SEQ).astype(jnp.int32)
    upper = 2 * N_SEQ - 1 - lower
    return jnp.stack([lower, upper], axis=1).reshape(2 * N_SEQ).astype(jnp.int32)


def level_of(stream_key, shape, cuts, least, largest):
    level = 1.0
    for position, blocks in cuts:
        heights = jax.random.uniform(jax.random.fold_in(jax.random.fold_in(stream_key, 6), position), (blocks,), jnp.float32, least / len(cuts), largest / len(cuts))
        level = level * jnp.repeat(jnp.exp(heights), shape[position] // blocks).reshape((-1,) + (1,) * (len(shape) - 1 - position))
    return level


def noise(own_key, shape, deviation, reach, shards=(), held_as=jnp.bfloat16):
    result = jax.random.normal(own_key, shape, jnp.float32) * deviation
    if len(shards) > 0:
        result = level_of(own_key, shape, shards, -0.22, 0.18) * result
    return jnp.clip(result, min=-reach, max=reach).astype(held_as)


def setup_inputs(seed: int = 0) -> dict:
    key_of = jax.random.split(jax.random.key(seed), 7)
    return {
        "tokens": draw_tokens(jax.random.fold_in(key_of[6], 71), 0),
        "block_order": draw_block_order(jax.random.fold_in(key_of[6], 71), 0),
        "query_weight": noise(key_of[2], (D, H * HD), D ** -0.5, 0.09375, ((0, 2), (1, 8))),
        "key_weight": noise(key_of[3], (D, KV * HD), D ** -0.5, 0.09375, ((0, 2), (1, 8))),
        "value_weight": noise(key_of[4], (D, KV * HD), D ** -0.5, 0.09375, ((0, 2), (1, 8))),
        "output_weight": noise(key_of[5], (H * HD, D), (H * HD) ** -0.5, 0.09375, ((0, 8),)),
    }


rope_theta = 500000.0
large_negative = -1e30


def rotate(vectors, positions):
    half_width = vectors.shape[-1] // 2
    freqs = rope_theta ** (-(jnp.arange(half_width, dtype=jnp.float32) * 2.0 / vectors.shape[-1]))
    angles = positions.astype(jnp.float32)[:, None] * freqs[None, :]
    cosine = jnp.cos(angles)[:, None, :]
    sine = jnp.sin(angles)[:, None, :]
    first = vectors[..., :half_width]
    second = vectors[..., half_width:]
    return jnp.concatenate([first * cosine - second * sine, second * cosine + first * sine], axis=-1)


def token_positions(block_order, first_row, count, half_rows):
    rows_index = first_row + jnp.arange(count, dtype=jnp.int32)
    slots = rows_index // half_rows
    matched = slots[:, None] == jnp.arange(block_order.shape[0], dtype=jnp.int32)[None, :]
    chosen = jnp.sum(jnp.where(matched, block_order[None, :], 0), axis=1).astype(jnp.int32)
    return chosen * half_rows + rows_index % half_rows


def reference(tokens, block_order, query_weight, key_weight, value_weight, output_weight):
    total = tokens.shape[0]
    half_rows = TOK_DEV // 2
    positions = token_positions(block_order, 0, total, half_rows)
    queries = jnp.dot(tokens, query_weight, preferred_element_type=jnp.float32).reshape(total, H, HD)
    keys_all = jnp.dot(tokens, key_weight, preferred_element_type=jnp.float32).reshape(total, KV, HD)
    values_all = jnp.dot(tokens, value_weight, preferred_element_type=jnp.float32).reshape(total, KV, HD)
    queries = rotate(queries, positions).astype(jnp.bfloat16)
    keys_all = rotate(keys_all, positions).astype(jnp.bfloat16)
    values_all = values_all.astype(jnp.bfloat16)
    group_size = H // KV
    block_rows = min(total, 1024)
    blocks = total // block_rows
    grouped = queries.reshape(blocks, block_rows, KV, group_size, HD).transpose(2, 0, 1, 3, 4)
    query_pos = positions.reshape(blocks, block_rows)
    score_scale = HD ** -0.5

    def per_head(inputs):
        head_queries, head_keys, head_values = inputs
        keys_wide = head_keys.astype(jnp.float32)
        values_wide = head_values.astype(jnp.float32)

        def per_block(block_inputs):
            block_queries, block_pos = block_inputs
            scores = jnp.einsum("qhd,kd->qhk", block_queries.astype(jnp.float32), keys_wide) * score_scale
            visible = positions[None, None, :] <= block_pos[:, None, None]
            scores = jnp.where(visible, scores, large_negative)
            highest = jnp.max(scores, axis=-1, keepdims=True)
            weights = jnp.where(visible, jnp.exp(scores - highest), 0.0)
            denom = jnp.sum(weights, axis=-1)
            rounded = lax.optimization_barrier(weights.astype(jnp.bfloat16))
            mixed = jnp.einsum("qhk,kd->qhd", rounded.astype(jnp.float32), values_wide)
            return (mixed / denom[..., None]).astype(jnp.bfloat16)

        return lax.map(per_block, (head_queries, query_pos))

    attended = lax.map(per_head, (grouped, keys_all.transpose(1, 0, 2), values_all.transpose(1, 0, 2)))
    attended = attended.transpose(1, 2, 0, 3, 4).reshape(total, H * HD)
    return jnp.dot(attended, output_weight, preferred_element_type=jnp.float32)
```

```python
from functools import partial

import jax
import jax.numpy as jnp
from jax import lax
from jax.experimental import pallas as pl
from jax.experimental.pallas import tpu as pltpu
from jax.sharding import Mesh, PartitionSpec as P

HD = 128
rope_theta = 500000.0
large_negative = -1e30
score_to_log2 = float(HD**-0.5 * 1.4426950408889634)
f32 = jnp.float32
bf16 = jnp.bfloat16
VMEM = pl.BlockSpec(memory_space=pltpu.VMEM)
SMEM = pl.BlockSpec(memory_space=pltpu.SMEM)
HBM = pl.BlockSpec(memory_space=pltpu.HBM)


def params(kib):
    return pltpu.CompilerParams(vmem_limit_bytes=kib * 1024)


def dot_t(a, b):
    return lax.dot_general(a, b, (((1,), (1,)), ((), ())), preferred_element_type=f32)


def place():
    return lax.axis_index("yh"), lax.axis_index("z"), lax.axis_index("row")


def project_kernel(
    peers, order_ref, freq_ref, tok_ref, qw_ref, kw_ref, vw_ref, own_ref, send_ref, angle_ref, tok, weight, acc, sems
):
    q_width = qw_ref.shape[1]
    depth = tok_ref.shape[1]
    chunks = sems.shape[0]
    blk = depth // chunks
    copies = []
    for c in range(chunks):
        at = slice(c * blk, (c + 1) * blk)
        pairs = (
            (tok_ref.at[:, at], tok.at[:, at]),
            (qw_ref.at[at], weight.at[at, :q_width]),
            (kw_ref.at[at], weight.at[at, q_width : q_width + HD]),
            (vw_ref.at[at], weight.at[at, q_width + HD :]),
        )
        copies.append([pltpu.make_async_copy(*pair, sems.at[c, k]) for k, pair in enumerate(pairs)])
        for copy in copies[-1]:
            copy.start()

    yh, z, row = place()
    half = acc.shape[0] // 2
    part = half // 2
    index = lax.broadcasted_iota(jnp.int32, angle_ref.shape, 0)
    slot = 2 * (yh * peers + z)
    block = jnp.where(index < part, order_ref[slot], order_ref[slot + 1])
    position = block * half + row * part + (index & (part - 1))
    angle_ref[...] = position.astype(f32) * freq_ref[...]

    for c in range(chunks):
        at = slice(c * blk, (c + 1) * blk)
        for copy in copies[c]:
            copy.wait()
        product = jnp.dot(tok[:, at], weight[at], preferred_element_type=f32)
        acc[...] = product if c == 0 else acc[...] + product

    for k in range(2):
        mine = pl.ds(pl.multiple_of(k * half + row * part, part), part)
        theirs = pl.ds(pl.multiple_of(k * half + (1 - row) * part, part), part)
        own_ref[k * part : (k + 1) * part, :] = acc[mine, :]
        send_ref[k * part : (k + 1) * part, :] = acc[theirs, :]


def project(order, freqs, tokens, query_weight, key_weight, value_weight):
    rows, depth = tokens.shape
    width = query_weight.shape[1] + 2 * HD
    chunks = 4
    out = jax.ShapeDtypeStruct((rows // 2, width), f32)
    return pl.pallas_call(
        partial(project_kernel, lax.axis_size("z")),
        in_specs=[SMEM, VMEM] + [HBM] * 4,
        out_specs=[VMEM] * 3,
        out_shape=[out, out, jax.ShapeDtypeStruct((rows // 2, HD), f32)],
        scratch_shapes=[
            pltpu.VMEM((rows, depth), bf16),
            pltpu.VMEM((depth, width), bf16),
            pltpu.VMEM((rows, width), f32),
            pltpu.SemaphoreType.DMA((chunks, 4)),
        ],
        compiler_params=params(60000),
        name="project",
    )(order, freqs, tokens, query_weight, key_weight, value_weight)


def rope_kernel(own_ref, recv_ref, cos_ref, sin_ref, q_ref, kv_ref):
    cosine = cos_ref[...]
    lane = lax.broadcasted_iota(jnp.int32, sin_ref.shape, 1)
    sine = jnp.where(lane < HD // 2, -sin_ref[...], sin_ref[...])
    heads = q_ref.shape[1] // HD
    for h in range(heads + 1):
        cols = slice(h * HD, (h + 1) * HD)
        x = own_ref[:, cols] + recv_ref[:, cols]
        y = (x * cosine + pltpu.roll(x, HD // 2, 1) * sine).astype(bf16)
        if h < heads:
            q_ref[:, cols] = y
        else:
            kv_ref[:, :HD] = y
    cols = slice((heads + 1) * HD, (heads + 2) * HD)
    kv_ref[:, HD:] = (own_ref[:, cols] + recv_ref[:, cols]).astype(bf16)


def attend_kernel(order_ref, q_ref, own_ref, other_ref, ow_hbm, out_ref, ow_ref, sem):
    fetch = pltpu.make_async_copy(ow_hbm, ow_ref, sem)
    fetch.start()
    yh, z, row = place()
    peers_a, tok, width = q_ref.shape
    peers_e = own_ref.shape[0]
    part = tok // 2
    heads = width // HD
    rows = heads * part
    keys = peers_e * part

    lane = lax.broadcasted_iota(jnp.int32, (1, keys), 1)
    low_base = jnp.zeros((1, keys), jnp.int32)
    high_base = jnp.zeros((1, keys), jnp.int32)
    for e in range(peers_e):
        at = (lane >= e * part) & (lane < (e + 1) * part)
        slot = 2 * (yh * peers_e + e)
        low_base = jnp.where(at, order_ref[slot], low_base)
        high_base = jnp.where(at, order_ref[slot + 1], high_base)
    inner = lane & (part - 1)

    def side(base, core):
        return base * (2 * part) + inner + core * part

    low_pos = jnp.concatenate([side(low_base, row), side(low_base, 1 - row)], axis=1)
    high_pos = jnp.concatenate([side(high_base, row), side(high_base, 1 - row)], axis=1)

    def both(first, last, c0):
        pieces = [
            ref[:, first:last, c0 : c0 + HD].reshape(keys, HD) for ref in (own_ref, other_ref)
        ]
        return jnp.concatenate(pieces, axis=0)

    k_low, v_low = both(0, part, 0), both(0, part, HD)
    k_high, v_high = both(part, tok, 0), both(part, tok, HD)
    q_inner = lax.broadcasted_iota(jnp.int32, (rows, 1), 0) & (part - 1)
    spot = lax.broadcasted_iota(jnp.int32, (rows, HD), 1)

    for a in range(peers_a):
        slot = 2 * (a * peers_e + z)

        def stacked(first, last):
            return jnp.concatenate(
                [q_ref[a, first:last, h * HD : (h + 1) * HD] for h in range(heads)], axis=0
            )

        q_low, q_high = stacked(0, part), stacked(part, tok)
        q_low_pos = order_ref[slot] * (2 * part) + row * part + q_inner
        q_high_pos = order_ref[slot + 1] * (2 * part) + row * part + q_inner

        s_ll = jnp.where(low_pos <= q_low_pos, dot_t(q_low, k_low), large_negative)
        m_low = jnp.maximum(jnp.max(s_ll, axis=1, keepdims=True), large_negative * 0.1)
        p_ll = jnp.exp2((s_ll - m_low) * score_to_log2)
        d_low = jnp.sum(p_ll, axis=1, keepdims=True)
        o_low = jnp.dot(p_ll.astype(bf16), v_low, preferred_element_type=f32)

        s_hl = dot_t(q_high, k_low)
        s_hh = jnp.where(high_pos <= q_high_pos, dot_t(q_high, k_high), large_negative)
        m_high = jnp.maximum(
            jnp.max(s_hl, axis=1, keepdims=True), jnp.max(s_hh, axis=1, keepdims=True)
        )
        p_hl = jnp.exp2((s_hl - m_high) * score_to_log2)
        p_hh = jnp.exp2((s_hh - m_high) * score_to_log2)
        d_high = jnp.sum(p_hl, axis=1, keepdims=True) + jnp.sum(p_hh, axis=1, keepdims=True)
        o_high = jnp.dot(p_hl.astype(bf16), v_low, preferred_element_type=f32) + jnp.dot(
            p_hh.astype(bf16), v_high, preferred_element_type=f32
        )

        logs = jnp.zeros((rows, HD), f32)
        for i, (m, d, o) in enumerate(((m_low, d_low, o_low), (m_high, d_high, o_high))):
            seen = d > 0.0
            safe = jnp.where(seen, d, 1.0)
            out_ref[a, i * rows : (i + 1) * rows, :] = (o / safe).astype(bf16)
            log = jnp.where(seen, m * score_to_log2 + jnp.log2(safe), large_negative)
            for j in range(3):
                piece = log.astype(bf16).astype(f32)
                logs = jnp.where(spot == 3 * i + j, piece, logs)
                log = log - piece
        out_ref[a, 2 * rows :, :] = logs.T[:16, :].astype(bf16)
    fetch.wait()


def output_kernel(parts_ref, ow_ref, out_ref, att):
    peers, _, _ = parts_ref.shape
    tok, width = att.shape
    part = tok // 2
    heads = width // HD
    rows = heads * part

    shares = []
    for i in range(2):
        logs = []
        for p in range(peers):
            got = parts_ref[p, 2 * rows : 2 * rows + 16, :].astype(f32)
            logs.append(got[3 * i : 3 * i + 1] + got[3 * i + 1 : 3 * i + 2] + got[3 * i + 2 : 3 * i + 3])
        top = logs[0]
        for log in logs[1:]:
            top = jnp.maximum(top, log)
        weights = [jnp.exp2(log - top) for log in logs]
        total = weights[0]
        for w in weights[1:]:
            total = total + w
        shares += [w / total for w in weights]
    filled = jnp.concatenate(shares + [jnp.zeros((HD - 2 * peers, rows), f32)], axis=0)
    columns = filled.T
    for i in range(2):
        joined = jnp.zeros((rows, HD), f32)
        for p in range(peers):
            at = i * peers + p
            got = parts_ref[p, i * rows : (i + 1) * rows, :].astype(f32)
            joined += columns[:, at : at + 1] * got
        joined = joined.astype(bf16)
        for h in range(heads):
            att[i * part : (i + 1) * part, h * HD : (h + 1) * HD] = joined[h * part : (h + 1) * part, :]

    size = out_ref.shape[2]
    for k in range(out_ref.shape[0]):
        cols = slice(k * size, (k + 1) * size)
        out_ref[k] = jnp.dot(att[...], ow_ref[:, cols], preferred_element_type=f32).astype(bf16)


def output(parts, output_weight, tok, peers):
    width, columns = output_weight.shape
    return pl.pallas_call(
        output_kernel,
        in_specs=[VMEM] * 2,
        out_specs=VMEM,
        out_shape=jax.ShapeDtypeStruct((peers, tok, columns // peers), bf16),
        scratch_shapes=[pltpu.VMEM((tok, width), bf16)],
        compiler_params=params(12288),
        name="output",
    )(parts, output_weight)


def gather_kernel(recv_ref, out_ref):
    part = recv_ref.shape[1] // 2
    peers = recv_ref.shape[0] // 2
    for core in range(2):
        total = recv_ref[core * peers].astype(f32)
        for c in range(1, peers):
            total = total + recv_ref[core * peers + c].astype(f32)
        for k in range(2):
            at = 2 * k * part + core * part
            out_ref[at : at + part, :] = total[k * part : (k + 1) * part, :]


def body(tokens, block_order, query_weight, key_weight, value_weight, output_weight):
    rows_here = tokens.shape[0]
    tok = rows_here // 2
    part = tok // 2
    q_width = query_weight.shape[1]

    half_width = HD // 2
    freqs = rope_theta ** (-(jnp.arange(half_width, dtype=f32) * 2.0 / HD))
    freqs = jnp.concatenate([freqs, freqs])[None]
    own, send, angles = project(block_order, freqs, tokens, query_weight, key_weight, value_weight)
    recv = lax.ppermute(send, "row", [(0, 1), (1, 0)])

    queries, key_values = pl.pallas_call(
        rope_kernel,
        in_specs=[VMEM] * 4,
        out_specs=[VMEM] * 2,
        out_shape=[
            jax.ShapeDtypeStruct((tok, q_width), bf16),
            jax.ShapeDtypeStruct((tok, 2 * HD), bf16),
        ],
        compiler_params=params(8192),
        name="rope",
    )(own, recv, jnp.cos(angles), jnp.sin(angles))

    peers_a = lax.axis_size("yh")
    spread = jnp.broadcast_to(queries[None], (peers_a, tok, q_width))
    all_queries = lax.all_to_all(spread, "yh", 0, 0)
    own_keys = lax.all_gather(key_values, "z")
    other_keys = lax.ppermute(own_keys, "row", [(0, 1), (1, 0)])

    heads = q_width // HD
    result, fetched = pl.pallas_call(
        attend_kernel,
        in_specs=[SMEM, VMEM, VMEM, VMEM, HBM],
        out_specs=[VMEM] * 2,
        out_shape=[
            jax.ShapeDtypeStruct((peers_a, 2 * heads * part + 16, HD), bf16),
            jax.ShapeDtypeStruct(output_weight.shape, bf16),
        ],
        scratch_shapes=[pltpu.SemaphoreType.DMA],
        compiler_params=params(48000),
        name="attend",
    )(block_order, all_queries, own_keys, other_keys, output_weight)

    parts = lax.all_to_all(result, "yh", 0, 0)
    across = ("row", "x", "yl")
    partial_out = output(parts, fetched, tok, lax.axis_size(across))
    shares = lax.all_to_all(partial_out, across, 0, 0)
    return pl.pallas_call(
        gather_kernel,
        in_specs=[VMEM],
        out_specs=VMEM,
        out_shape=jax.ShapeDtypeStruct((rows_here, shares.shape[2]), f32),
        compiler_params=params(8192),
        name="gather",
    )(shares)


def solution(mesh):
    seq, row, col = (mesh.shape[name] for name in ("seq", "row", "col"))
    z = min(16, seq // 2)
    yl = 2 if col == 8 else 1
    devices = mesh.devices.reshape(seq // z, z, row, col // yl, yl)
    fine = Mesh(devices, ("yh", "z", "row", "x", "yl"))
    seq_axes, col_axes = ("yh", "z"), ("x", "yl")
    placed = (
        P(seq_axes, "row"),
        P(),
        P("row", col_axes),
        P("row", col_axes),
        P("row", col_axes),
        P(col_axes, None),
    )
    return jax.shard_map(
        body,
        mesh=fine,
        in_specs=placed,
        out_specs=P(seq_axes, ("row", *col_axes)),
        check_vma=False,
    )
```

```python
from functools import partial

import jax
import jax.numpy as jnp
from jax import lax
from jax.experimental import pallas as pl
from jax.experimental.pallas import tpu as pltpu
from jax.sharding import Mesh, PartitionSpec as P

HD = 128
rope_theta = 500000.0
large_negative = -1e30
score_to_log2 = float(HD**-0.5 * 1.4426950408889634)
f32 = jnp.float32
bf16 = jnp.bfloat16
VMEM = pl.BlockSpec(memory_space=pltpu.VMEM)
SMEM = pl.BlockSpec(memory_space=pltpu.SMEM)
HBM = pl.BlockSpec(memory_space=pltpu.HBM)


def params(kib):
    return pltpu.CompilerParams(vmem_limit_bytes=kib * 1024)


def dot_t(a, b):
    return lax.dot_general(a, b, (((1,), (1,)), ((), ())), preferred_element_type=f32)


def place():
    return lax.axis_index("yh"), lax.axis_index("z"), lax.axis_index("row")


def project_kernel(
    peers, order_ref, freq_ref, tok_ref, qw_ref, kw_ref, vw_ref, own_ref, send_ref, angle_ref, tok, weight, acc, sems
):
    q_width = qw_ref.shape[1]
    depth = tok_ref.shape[1]
    chunks = sems.shape[0]
    blk = depth // chunks
    copies = []
    for c in range(chunks):
        at = slice(c * blk, (c + 1) * blk)
        pairs = (
            (tok_ref.at[:, at], tok.at[:, at]),
            (qw_ref.at[at], weight.at[at, :q_width]),
            (kw_ref.at[at], weight.at[at, q_width : q_width + HD]),
            (vw_ref.at[at], weight.at[at, q_width + HD :]),
        )
        copies.append([pltpu.make_async_copy(*pair, sems.at[c, k]) for k, pair in enumerate(pairs)])
        for copy in copies[-1]:
            copy.start()

    yh, z, row = place()
    half = acc.shape[0] // 2
    part = half // 2
    index = lax.broadcasted_iota(jnp.int32, angle_ref.shape, 0)
    slot = 2 * (yh * peers + z)
    block = jnp.where(index < part, order_ref[slot], order_ref[slot + 1])
    position = block * half + row * part + (index & (part - 1))
    angle_ref[...] = position.astype(f32) * freq_ref[...]

    for c in range(chunks):
        at = slice(c * blk, (c + 1) * blk)
        for copy in copies[c]:
            copy.wait()
        product = jnp.dot(tok[:, at], weight[at], preferred_element_type=f32)
        acc[...] = product if c == 0 else acc[...] + product

    for k in range(2):
        mine = pl.ds(pl.multiple_of(k * half + row * part, part), part)
        theirs = pl.ds(pl.multiple_of(k * half + (1 - row) * part, part), part)
        own_ref[k * part : (k + 1) * part, :] = acc[mine, :]
        send_ref[k * part : (k + 1) * part, :] = acc[theirs, :]


def project(order, freqs, tokens, query_weight, key_weight, value_weight):
    rows, depth = tokens.shape
    width = query_weight.shape[1] + 2 * HD
    chunks = 4
    out = jax.ShapeDtypeStruct((rows // 2, width), f32)
    return pl.pallas_call(
        partial(project_kernel, lax.axis_size("z")),
        in_specs=[SMEM, VMEM] + [HBM] * 4,
        out_specs=[VMEM] * 3,
        out_shape=[out, out, jax.ShapeDtypeStruct((rows // 2, HD), f32)],
        scratch_shapes=[
            pltpu.VMEM((rows, depth), bf16),
            pltpu.VMEM((depth, width), bf16),
            pltpu.VMEM((rows, width), f32),
            pltpu.SemaphoreType.DMA((chunks, 4)),
        ],
        compiler_params=params(16384),
        name="project",
    )(order, freqs, tokens, query_weight, key_weight, value_weight)


def rope_kernel(own_ref, recv_ref, cos_ref, sin_ref, q_ref, kv_ref):
    cosine = cos_ref[...]
    lane = lax.broadcasted_iota(jnp.int32, sin_ref.shape, 1)
    sine = jnp.where(lane < HD // 2, -sin_ref[...], sin_ref[...])
    heads = q_ref.shape[1] // HD
    for h in range(heads + 1):
        cols = slice(h * HD, (h + 1) * HD)
        x = own_ref[:, cols] + recv_ref[:, cols]
        y = (x * cosine + pltpu.roll(x, HD // 2, 1) * sine).astype(bf16)
        if h < heads:
            q_ref[:, cols] = y
        else:
            kv_ref[:, :HD] = y
    cols = slice((heads + 1) * HD, (heads + 2) * HD)
    kv_ref[:, HD:] = (own_ref[:, cols] + recv_ref[:, cols]).astype(bf16)


def attend_kernel(order_ref, q_ref, own_ref, other_ref, ow_hbm, out_ref, ow_ref, sem):
    fetch = pltpu.make_async_copy(ow_hbm, ow_ref, sem)
    fetch.start()
    yh, z, row = place()
    peers_a, tok, width = q_ref.shape
    peers_e = own_ref.shape[0]
    part = tok // 2
    heads = width // HD
    rows = heads * part
    keys = peers_e * part

    lane = lax.broadcasted_iota(jnp.int32, (1, keys), 1)
    low_base = jnp.zeros((1, keys), jnp.int32)
    high_base = jnp.zeros((1, keys), jnp.int32)
    for e in range(peers_e):
        at = (lane >= e * part) & (lane < (e + 1) * part)
        slot = 2 * (yh * peers_e + e)
        low_base = jnp.where(at, order_ref[slot], low_base)
        high_base = jnp.where(at, order_ref[slot + 1], high_base)
    inner = lane & (part - 1)

    def side(base, core):
        return base * (2 * part) + inner + core * part

    low_pos = jnp.concatenate([side(low_base, row), side(low_base, 1 - row)], axis=1)
    high_pos = jnp.concatenate([side(high_base, row), side(high_base, 1 - row)], axis=1)

    def both(first, last, c0):
        pieces = [
            ref[:, first:last, c0 : c0 + HD].reshape(keys, HD) for ref in (own_ref, other_ref)
        ]
        return jnp.concatenate(pieces, axis=0)

    ones = jnp.where(lax.broadcasted_iota(jnp.int32, (2 * keys, HD), 1) == 0, 1.0, 0.0).astype(bf16)
    k_low, k_high = both(0, part, 0), both(part, tok, 0)
    v_low = jnp.concatenate([both(0, part, HD), ones], axis=1)
    v_high = jnp.concatenate([both(part, tok, HD), ones], axis=1)
    q_inner = lax.broadcasted_iota(jnp.int32, (rows, 1), 0) & (part - 1)
    spot = lax.broadcasted_iota(jnp.int32, (rows, HD), 1)

    for turn in range(peers_a):
        a = (yh + turn) & (peers_a - 1)
        slot = 2 * (a * peers_e + z)
        b_low, b_high = order_ref[slot], order_ref[slot + 1]
        mine = q_ref.at[a]

        def stacked(first, last):
            return [mine[first:last, h * HD : (h + 1) * HD] for h in range(heads)]

        q_both = jnp.concatenate(stacked(0, part) + stacked(part, tok), axis=0)
        s_low = dot_t(q_both, k_low)
        s_ll, s_hl = s_low[:rows], s_low[rows:]
        s_hh = dot_t(q_both[rows:], k_high)
        if turn == 0:
            s_ll = jnp.where(low_pos <= b_low * (2 * part) + row * part + q_inner, s_ll, large_negative)
            s_hh = jnp.where(high_pos <= b_high * (2 * part) + row * part + q_inner, s_hh, large_negative)
        else:
            s_ll = s_ll + jnp.where(low_pos < b_low * (2 * part), 0.0, large_negative)
            s_hh = s_hh + jnp.where(high_pos < b_high * (2 * part), 0.0, large_negative)
        m_low = jnp.maximum(jnp.max(s_ll, axis=1, keepdims=True), large_negative * 0.1)
        m_high = jnp.maximum(
            jnp.max(s_hl, axis=1, keepdims=True), jnp.max(s_hh, axis=1, keepdims=True)
        )
        p_ll = jnp.exp2((s_ll - m_low) * score_to_log2).astype(bf16)
        p_hl = jnp.exp2((s_hl - m_high) * score_to_log2).astype(bf16)
        p_hh = jnp.exp2((s_hh - m_high) * score_to_log2).astype(bf16)
        o_both = jnp.dot(jnp.concatenate([p_ll, p_hl], axis=0), v_low, preferred_element_type=f32)
        o_low = o_both[:rows]
        o_high = o_both[rows:] + jnp.dot(p_hh, v_high, preferred_element_type=f32)

        logs = jnp.zeros((rows, HD), f32)
        for i, (m, o) in enumerate(((m_low, o_low), (m_high, o_high))):
            d = o[:, HD : HD + 1]
            seen = d > 0.0
            safe = jnp.where(seen, d, 1.0)
            out_ref[a, i * rows : (i + 1) * rows, :] = (o[:, :HD] * (1.0 / safe)).astype(bf16)
            log = jnp.where(seen, m * score_to_log2 + jnp.log2(safe), large_negative)
            for j in range(3):
                piece = log.astype(bf16).astype(f32)
                logs = jnp.where(spot == 3 * i + j, piece, logs)
                log = log - piece
        out_ref[a, 2 * rows :, :] = logs.T[:16, :].astype(bf16)
    fetch.wait()


def attend(block_order, queries, own_keys, other_keys, output_weight):
    peers, tok, width = queries.shape
    return pl.pallas_call(
        attend_kernel,
        in_specs=[SMEM, VMEM, VMEM, VMEM, HBM],
        out_specs=[VMEM] * 2,
        out_shape=[
            jax.ShapeDtypeStruct((peers, tok * width // HD + 16, HD), bf16),
            jax.ShapeDtypeStruct(output_weight.shape, bf16),
        ],
        scratch_shapes=[pltpu.SemaphoreType.DMA],
        compiler_params=params(24576),
        name="attend",
    )(block_order, queries, own_keys, other_keys, output_weight)


def output_kernel(parts_ref, ow_ref, out_ref, att):
    peers, _, _ = parts_ref.shape
    tok, width = att.shape
    part = tok // 2
    heads = width // HD
    rows = heads * part

    shares = []
    for i in range(2):
        logs = []
        for p in range(peers):
            got = parts_ref[p, 2 * rows : 2 * rows + 16, :].astype(f32)
            logs.append(got[3 * i : 3 * i + 1] + got[3 * i + 1 : 3 * i + 2] + got[3 * i + 2 : 3 * i + 3])
        top = logs[0]
        for log in logs[1:]:
            top = jnp.maximum(top, log)
        weights = [jnp.exp2(log - top) for log in logs]
        total = weights[0]
        for w in weights[1:]:
            total = total + w
        shares += [w / total for w in weights]
    filled = jnp.concatenate(shares + [jnp.zeros((HD - 2 * peers, rows), f32)], axis=0)
    columns = filled.T
    for i in range(2):
        joined = jnp.zeros((rows, HD), f32)
        for p in range(peers):
            at = i * peers + p
            got = parts_ref[p, i * rows : (i + 1) * rows, :].astype(f32)
            joined += columns[:, at : at + 1] * got
        joined = joined.astype(bf16)
        for h in range(heads):
            att[i * part : (i + 1) * part, h * HD : (h + 1) * HD] = joined[h * part : (h + 1) * part, :]

    size = out_ref.shape[2]
    for k in range(out_ref.shape[0]):
        cols = slice(k * size, (k + 1) * size)
        out_ref[k] = jnp.dot(att[...], ow_ref[:, cols], preferred_element_type=f32).astype(bf16)


def output(parts, output_weight, tok, peers):
    width, columns = output_weight.shape
    return pl.pallas_call(
        output_kernel,
        in_specs=[VMEM] * 2,
        out_specs=VMEM,
        out_shape=jax.ShapeDtypeStruct((peers, tok, columns // peers), bf16),
        scratch_shapes=[pltpu.VMEM((tok, width), bf16)],
        compiler_params=params(12288),
        name="output",
    )(parts, output_weight)


def gather_kernel(recv_ref, out_ref):
    part = recv_ref.shape[1] // 2
    peers = recv_ref.shape[0] // 2
    for core in range(2):
        total = recv_ref[core * peers].astype(f32)
        for c in range(1, peers):
            total = total + recv_ref[core * peers + c].astype(f32)
        for k in range(2):
            at = 2 * k * part + core * part
            out_ref[at : at + part, :] = total[k * part : (k + 1) * part, :]


def body(tokens, block_order, query_weight, key_weight, value_weight, output_weight):
    rows_here = tokens.shape[0]
    tok = rows_here // 2
    q_width = query_weight.shape[1]

    half_width = HD // 2
    freqs = rope_theta ** (-(jnp.arange(half_width, dtype=f32) * 2.0 / HD))
    freqs = jnp.concatenate([freqs, freqs])[None]
    block_order, tokens, query_weight, key_weight, value_weight, output_weight = (
        pltpu.with_memory_space_constraint(array, pltpu.HBM)
        for array in (block_order, tokens, query_weight, key_weight, value_weight, output_weight)
    )
    own, send, angles = project(block_order, freqs, tokens, query_weight, key_weight, value_weight)
    recv = lax.ppermute(send, "row", [(0, 1), (1, 0)])

    queries, key_values = pl.pallas_call(
        rope_kernel,
        in_specs=[VMEM] * 4,
        out_specs=[VMEM] * 2,
        out_shape=[
            jax.ShapeDtypeStruct((tok, q_width), bf16),
            jax.ShapeDtypeStruct((tok, 2 * HD), bf16),
        ],
        compiler_params=params(8192),
        name="rope",
    )(own, recv, jnp.cos(angles), jnp.sin(angles))

    peers_a = lax.axis_size("yh")
    spread = jnp.broadcast_to(queries[None], (peers_a, tok, q_width))
    all_queries = lax.all_to_all(spread, "yh", 0, 0)
    own_keys = lax.all_gather(key_values, "z")
    other_keys = lax.ppermute(own_keys, "row", [(0, 1), (1, 0)])

    result, fetched = attend(block_order, all_queries, own_keys, other_keys, output_weight)
    parts = lax.all_to_all(result, "yh", 0, 0)
    across = ("row", "x", "yl")
    partial_out = output(parts, fetched, tok, lax.axis_size(across))
    shares = lax.all_to_all(partial_out, across, 0, 0)
    return pl.pallas_call(
        gather_kernel,
        in_specs=[VMEM],
        out_specs=VMEM,
        out_shape=jax.ShapeDtypeStruct((rows_here, shares.shape[2]), f32),
        compiler_params=params(8192),
        name="gather",
    )(shares)


def solution(mesh):
    seq, row, col = (mesh.shape[name] for name in ("seq", "row", "col"))
    z = min(16, seq // 2)
    yl = 2 if col == 8 else 1
    devices = mesh.devices.reshape(seq // z, z, row, col // yl, yl)
    fine = Mesh(devices, ("yh", "z", "row", "x", "yl"))
    seq_axes, col_axes = ("yh", "z"), ("x", "yl")
    placed = (
        P(seq_axes, "row"),
        P(),
        P("row", col_axes),
        P("row", col_axes),
        P("row", col_axes),
        P(col_axes, None),
    )
    return jax.shard_map(
        body,
        mesh=fine,
        in_specs=placed,
        out_specs=P(seq_axes, ("row", *col_axes)),
        check_vma=False,
    )
```

```python
from functools import partial

import jax
import jax.numpy as jnp
from jax import lax
from jax.experimental import pallas as pl
from jax.experimental.pallas import tpu as pltpu
from jax.sharding import Mesh, PartitionSpec as P

HD = 128
rope_theta = 500000.0
large_negative = -1e30
score_to_log2 = float(HD**-0.5 * 1.4426950408889634)
f32 = jnp.float32
bf16 = jnp.bfloat16
VMEM = pl.BlockSpec(memory_space=pltpu.VMEM)
SMEM = pl.BlockSpec(memory_space=pltpu.SMEM)
HBM = pl.BlockSpec(memory_space=pltpu.HBM)


def params(kib):
    return pltpu.CompilerParams(vmem_limit_bytes=kib * 1024)


def dot_t(a, b):
    return lax.dot_general(a, b, (((1,), (1,)), ((), ())), preferred_element_type=f32)


def place():
    return lax.axis_index("yh"), lax.axis_index("z"), lax.axis_index("row")


def project_kernel(
    peers, order_ref, freq_ref, tok_ref, qw_ref, kw_ref, vw_ref, own_ref, send_ref, angle_ref, tok, weight, acc, sems
):
    q_width = qw_ref.shape[1]
    depth = tok_ref.shape[1]
    chunks = sems.shape[0]
    blk = depth // chunks
    copies = []
    for c in range(chunks):
        at = slice(c * blk, (c + 1) * blk)
        pairs = (
            (tok_ref.at[:, at], tok.at[:, at]),
            (qw_ref.at[at], weight.at[at, :q_width]),
            (kw_ref.at[at], weight.at[at, q_width : q_width + HD]),
            (vw_ref.at[at], weight.at[at, q_width + HD :]),
        )
        copies.append([pltpu.make_async_copy(*pair, sems.at[c, k]) for k, pair in enumerate(pairs)])
        for copy in copies[-1]:
            copy.start()

    yh, z, row = place()
    half = acc.shape[0] // 2
    part = half // 2
    index = lax.broadcasted_iota(jnp.int32, angle_ref.shape, 0)
    slot = 2 * (yh * peers + z)
    block = jnp.where(index < part, order_ref[slot], order_ref[slot + 1])
    position = block * half + row * part + (index & (part - 1))
    angle_ref[...] = position.astype(f32) * freq_ref[...]

    for c in range(chunks):
        at = slice(c * blk, (c + 1) * blk)
        for copy in copies[c]:
            copy.wait()
        product = jnp.dot(tok[:, at], weight[at], preferred_element_type=f32)
        acc[...] = product if c == 0 else acc[...] + product

    for k in range(2):
        mine = pl.ds(pl.multiple_of(k * half + row * part, part), part)
        theirs = pl.ds(pl.multiple_of(k * half + (1 - row) * part, part), part)
        own_ref[k * part : (k + 1) * part, :] = acc[mine, :]
        send_ref[k * part : (k + 1) * part, :] = acc[theirs, :]


def project(order, freqs, tokens, query_weight, key_weight, value_weight):
    rows, depth = tokens.shape
    width = query_weight.shape[1] + 2 * HD
    chunks = 4
    out = jax.ShapeDtypeStruct((rows // 2, width), f32)
    return pl.pallas_call(
        partial(project_kernel, lax.axis_size("z")),
        in_specs=[SMEM, VMEM] + [HBM] * 4,
        out_specs=[VMEM] * 3,
        out_shape=[out, out, jax.ShapeDtypeStruct((rows // 2, HD), f32)],
        scratch_shapes=[
            pltpu.VMEM((rows, depth), bf16),
            pltpu.VMEM((depth, width), bf16),
            pltpu.VMEM((rows, width), f32),
            pltpu.SemaphoreType.DMA((chunks, 4)),
        ],
        compiler_params=params(16384),
        name="project",
    )(order, freqs, tokens, query_weight, key_weight, value_weight)


def rope_kernel(own_ref, recv_ref, cos_ref, sin_ref, q_ref, kv_ref):
    cosine = cos_ref[...]
    lane = lax.broadcasted_iota(jnp.int32, sin_ref.shape, 1)
    sine = jnp.where(lane < HD // 2, -sin_ref[...], sin_ref[...])
    heads = q_ref.shape[1] // HD
    for h in range(heads + 1):
        cols = slice(h * HD, (h + 1) * HD)
        x = own_ref[:, cols] + recv_ref[:, cols]
        y = (x * cosine + pltpu.roll(x, HD // 2, 1) * sine).astype(bf16)
        if h < heads:
            q_ref[:, cols] = y
        else:
            for e in range(kv_ref.shape[0]):
                kv_ref[e, :, :HD] = y
    cols = slice((heads + 1) * HD, (heads + 2) * HD)
    y = (own_ref[:, cols] + recv_ref[:, cols]).astype(bf16)
    for e in range(kv_ref.shape[0]):
        kv_ref[e, :, HD:] = y


def attend_kernel(order_ref, q_ref, own_ref, other_ref, ow_hbm, out_ref, ow_ref, sem):
    fetch = pltpu.make_async_copy(ow_hbm, ow_ref, sem)
    fetch.start()
    yh, z, row = place()
    peers_a, tok, width = q_ref.shape
    peers_e = own_ref.shape[0]
    part = tok // 2
    heads = width // HD
    rows = heads * part
    keys = peers_e * part

    lane = lax.broadcasted_iota(jnp.int32, (1, keys), 1)
    low_base = jnp.zeros((1, keys), jnp.int32)
    high_base = jnp.zeros((1, keys), jnp.int32)
    for e in range(peers_e):
        at = (lane >= e * part) & (lane < (e + 1) * part)
        slot = 2 * (yh * peers_e + e)
        low_base = jnp.where(at, order_ref[slot], low_base)
        high_base = jnp.where(at, order_ref[slot + 1], high_base)
    inner = lane & (part - 1)

    def side(base, core):
        return base * (2 * part) + inner + core * part

    low_pos = jnp.concatenate([side(low_base, row), side(low_base, 1 - row)], axis=1)
    high_pos = jnp.concatenate([side(high_base, row), side(high_base, 1 - row)], axis=1)

    def both(first, last, c0):
        pieces = [
            ref[:, first:last, c0 : c0 + HD].reshape(keys, HD) for ref in (own_ref, other_ref)
        ]
        return jnp.concatenate(pieces, axis=0)

    ones = jnp.where(lax.broadcasted_iota(jnp.int32, (2 * keys, HD), 1) == 0, 1.0, 0.0).astype(bf16)
    k_low, k_high = both(0, part, 0), both(part, tok, 0)
    v_low = jnp.concatenate([both(0, part, HD), ones], axis=1)
    v_high = jnp.concatenate([both(part, tok, HD), ones], axis=1)
    q_inner = lax.broadcasted_iota(jnp.int32, (rows, 1), 0) & (part - 1)
    spot = lax.broadcasted_iota(jnp.int32, (rows, HD), 1)

    for turn in range(peers_a):
        a = (yh + turn) & (peers_a - 1)
        slot = 2 * (a * peers_e + z)
        b_low, b_high = order_ref[slot], order_ref[slot + 1]
        mine = q_ref.at[a]

        def stacked(first, last):
            return [mine[first:last, h * HD : (h + 1) * HD] for h in range(heads)]

        q_both = jnp.concatenate(stacked(0, part) + stacked(part, tok), axis=0)
        s_low = dot_t(q_both, k_low)
        s_ll, s_hl = s_low[:rows], s_low[rows:]
        s_hh = dot_t(q_both[rows:], k_high)
        if turn == 0:
            s_ll = jnp.where(low_pos <= b_low * (2 * part) + row * part + q_inner, s_ll, large_negative)
            s_hh = jnp.where(high_pos <= b_high * (2 * part) + row * part + q_inner, s_hh, large_negative)
        else:
            s_ll = s_ll + jnp.where(low_pos < b_low * (2 * part), 0.0, large_negative)
            s_hh = s_hh + jnp.where(high_pos < b_high * (2 * part), 0.0, large_negative)
        m_low = jnp.maximum(jnp.max(s_ll, axis=1, keepdims=True), large_negative * 0.1)
        m_high = jnp.maximum(
            jnp.max(s_hl, axis=1, keepdims=True), jnp.max(s_hh, axis=1, keepdims=True)
        )
        p_ll = jnp.exp2((s_ll - m_low) * score_to_log2).astype(bf16)
        p_hl = jnp.exp2((s_hl - m_high) * score_to_log2).astype(bf16)
        p_hh = jnp.exp2((s_hh - m_high) * score_to_log2).astype(bf16)
        o_both = jnp.dot(jnp.concatenate([p_ll, p_hl], axis=0), v_low, preferred_element_type=f32)
        o_low = o_both[:rows]
        o_high = o_both[rows:] + jnp.dot(p_hh, v_high, preferred_element_type=f32)

        logs = jnp.zeros((rows, HD), f32)
        for i, (m, o) in enumerate(((m_low, o_low), (m_high, o_high))):
            d = o[:, HD : HD + 1]
            seen = d > 0.0
            safe = jnp.where(seen, d, 1.0)
            out_ref[a, i * rows : (i + 1) * rows, :] = (o[:, :HD] * (1.0 / safe)).astype(bf16)
            log = jnp.where(seen, m * score_to_log2 + jnp.log2(safe), large_negative)
            for j in range(3):
                piece = log.astype(bf16).astype(f32)
                logs = jnp.where(spot == 3 * i + j, piece, logs)
                log = log - piece
        out_ref[a, 2 * rows :, :] = logs.T[:16, :].astype(bf16)
    fetch.wait()


def attend(block_order, queries, own_keys, other_keys, output_weight):
    peers, tok, width = queries.shape
    return pl.pallas_call(
        attend_kernel,
        in_specs=[SMEM, VMEM, VMEM, VMEM, HBM],
        out_specs=[VMEM] * 2,
        out_shape=[
            jax.ShapeDtypeStruct((peers, tok * width // HD + 16, HD), bf16),
            jax.ShapeDtypeStruct(output_weight.shape, bf16),
        ],
        scratch_shapes=[pltpu.SemaphoreType.DMA],
        compiler_params=params(24576),
        name="attend",
    )(block_order, queries, own_keys, other_keys, output_weight)


def output_kernel(parts_ref, ow_ref, out_ref, att):
    peers, _, _ = parts_ref.shape
    tok, width = att.shape
    part = tok // 2
    heads = width // HD
    rows = heads * part

    shares = []
    for i in range(2):
        logs = []
        for p in range(peers):
            got = parts_ref[p, 2 * rows : 2 * rows + 16, :].astype(f32)
            logs.append(got[3 * i : 3 * i + 1] + got[3 * i + 1 : 3 * i + 2] + got[3 * i + 2 : 3 * i + 3])
        top = logs[0]
        for log in logs[1:]:
            top = jnp.maximum(top, log)
        weights = [jnp.exp2(log - top) for log in logs]
        total = weights[0]
        for w in weights[1:]:
            total = total + w
        shares += [w / total for w in weights]
    filled = jnp.concatenate(shares + [jnp.zeros((HD - 2 * peers, rows), f32)], axis=0)
    columns = filled.T
    for i in range(2):
        joined = jnp.zeros((rows, HD), f32)
        for p in range(peers):
            at = i * peers + p
            got = parts_ref[p, i * rows : (i + 1) * rows, :].astype(f32)
            joined += columns[:, at : at + 1] * got
        joined = joined.astype(bf16)
        for h in range(heads):
            att[i * part : (i + 1) * part, h * HD : (h + 1) * HD] = joined[h * part : (h + 1) * part, :]

    size = out_ref.shape[2]
    for k in range(out_ref.shape[0]):
        cols = slice(k * size, (k + 1) * size)
        out_ref[k] = jnp.dot(att[...], ow_ref[:, cols], preferred_element_type=f32).astype(bf16)


def output(parts, output_weight, tok, peers):
    width, columns = output_weight.shape
    return pl.pallas_call(
        output_kernel,
        in_specs=[VMEM] * 2,
        out_specs=VMEM,
        out_shape=jax.ShapeDtypeStruct((peers, tok, columns // peers), bf16),
        scratch_shapes=[pltpu.VMEM((tok, width), bf16)],
        compiler_params=params(12288),
        name="output",
    )(parts, output_weight)


def gather_kernel(recv_ref, out_ref):
    part = recv_ref.shape[1] // 2
    peers = recv_ref.shape[0] // 2
    for core in range(2):
        total = recv_ref[core * peers].astype(f32)
        for c in range(1, peers):
            total = total + recv_ref[core * peers + c].astype(f32)
        for k in range(2):
            at = 2 * k * part + core * part
            out_ref[at : at + part, :] = total[k * part : (k + 1) * part, :]


def body(tokens, block_order, query_weight, key_weight, value_weight, output_weight):
    rows_here = tokens.shape[0]
    tok = rows_here // 2
    q_width = query_weight.shape[1]

    half_width = HD // 2
    freqs = rope_theta ** (-(jnp.arange(half_width, dtype=f32) * 2.0 / HD))
    freqs = jnp.concatenate([freqs, freqs])[None]
    block_order, tokens, query_weight, key_weight, value_weight, output_weight = (
        pltpu.with_memory_space_constraint(array, pltpu.HBM)
        for array in (block_order, tokens, query_weight, key_weight, value_weight, output_weight)
    )
    own, send, angles = project(block_order, freqs, tokens, query_weight, key_weight, value_weight)
    recv = lax.ppermute(send, "row", [(0, 1), (1, 0)])

    queries, key_values = pl.pallas_call(
        rope_kernel,
        in_specs=[VMEM] * 4,
        out_specs=[VMEM] * 2,
        out_shape=[
            jax.ShapeDtypeStruct((tok, q_width), bf16),
            jax.ShapeDtypeStruct((lax.axis_size("z"), tok, 2 * HD), bf16),
        ],
        compiler_params=params(8192),
        name="rope",
    )(own, recv, jnp.cos(angles), jnp.sin(angles))

    own_keys = lax.all_to_all(key_values, "z", 0, 0)
    all_queries = lax.all_gather(queries, "yh")
    other_keys = lax.ppermute(own_keys, "row", [(0, 1), (1, 0)])

    result, fetched = attend(block_order, all_queries, own_keys, other_keys, output_weight)
    parts = lax.all_to_all(result, "yh", 0, 0)
    across = ("row", "x", "yl")
    partial_out = output(parts, fetched, tok, lax.axis_size(across))
    shares = lax.all_to_all(partial_out, across, 0, 0)
    return pl.pallas_call(
        gather_kernel,
        in_specs=[VMEM],
        out_specs=VMEM,
        out_shape=jax.ShapeDtypeStruct((rows_here, shares.shape[2]), f32),
        compiler_params=params(8192),
        name="gather",
    )(shares)


def solution(mesh):
    seq, row, col = (mesh.shape[name] for name in ("seq", "row", "col"))
    z = min(16, seq // 2)
    yl = 2 if col == 8 else 1
    devices = mesh.devices.reshape(seq // z, z, row, col // yl, yl)
    fine = Mesh(devices, ("yh", "z", "row", "x", "yl"))
    seq_axes, col_axes = ("yh", "z"), ("x", "yl")
    placed = (
        P(seq_axes, "row"),
        P(),
        P("row", col_axes),
        P("row", col_axes),
        P("row", col_axes),
        P(col_axes, None),
    )
    return jax.shard_map(
        body,
        mesh=fine,
        in_specs=placed,
        out_specs=P(seq_axes, ("row", *col_axes)),
        check_vma=False,
    )
```

```python
from functools import partial

import jax
import jax.numpy as jnp
from jax import lax
from jax.experimental import pallas as pl
from jax.experimental.pallas import tpu as pltpu
from jax.sharding import Mesh, PartitionSpec as P

HD = 128
rope_theta = 500000.0
large_negative = -1e30
score_to_log2 = float(HD**-0.5 * 1.4426950408889634)
f32 = jnp.float32
bf16 = jnp.bfloat16
VMEM = pl.BlockSpec(memory_space=pltpu.VMEM)
SMEM = pl.BlockSpec(memory_space=pltpu.SMEM)
HBM = pl.BlockSpec(memory_space=pltpu.HBM)


def params(kib):
    return pltpu.CompilerParams(vmem_limit_bytes=kib * 1024)


def dot_t(a, b):
    return lax.dot_general(a, b, (((1,), (1,)), ((), ())), preferred_element_type=f32)


def place():
    return lax.axis_index("yh"), lax.axis_index("z"), lax.axis_index("row")


def project_kernel(peers, count, order_ref, freq_ref, tok_ref, *refs):
    weight_refs = refs[:count]
    own_ref, send_ref, angle_ref, tok, weight, acc, sems = refs[count:]
    depth = tok_ref.shape[1]
    chunks = sems.shape[0]
    blk = depth // chunks
    copies = []
    for c in range(chunks):
        at = slice(c * blk, (c + 1) * blk)
        pairs = [(tok_ref.at[:, at], tok.at[:, at])]
        first = 0
        for ref in weight_refs:
            pairs.append((ref.at[at], weight.at[at, first : first + ref.shape[1]]))
            first += ref.shape[1]
        copies.append([pltpu.make_async_copy(*pair, sems.at[c, k]) for k, pair in enumerate(pairs)])
        for copy in copies[-1]:
            copy.start()

    yh, z, row = place()
    half = acc.shape[0] // 2
    part = half // 2
    index = lax.broadcasted_iota(jnp.int32, angle_ref.shape, 0)
    slot = 2 * (yh * peers + z)
    block = jnp.where(index < part, order_ref[slot], order_ref[slot + 1])
    position = block * half + row * part + (index & (part - 1))
    angle_ref[...] = position.astype(f32) * freq_ref[...]

    for c in range(chunks):
        at = slice(c * blk, (c + 1) * blk)
        for copy in copies[c]:
            copy.wait()
        product = jnp.dot(tok[:, at], weight[at], preferred_element_type=f32)
        acc[...] = product if c == 0 else acc[...] + product

    for k in range(2):
        mine = pl.ds(pl.multiple_of(k * half + row * part, part), part)
        theirs = pl.ds(pl.multiple_of(k * half + (1 - row) * part, part), part)
        own_ref[k * part : (k + 1) * part, :] = acc[mine, :]
        send_ref[k * part : (k + 1) * part, :] = acc[theirs, :]


def project(order, freqs, tokens, *weights):
    rows, depth = tokens.shape
    width = sum(weight.shape[1] for weight in weights)
    chunks = 4
    out = jax.ShapeDtypeStruct((rows // 2, width), f32)
    return pl.pallas_call(
        partial(project_kernel, lax.axis_size("z"), len(weights)),
        in_specs=[SMEM, VMEM, HBM] + [HBM] * len(weights),
        out_specs=[VMEM] * 3,
        out_shape=[out, out, jax.ShapeDtypeStruct((rows // 2, HD), f32)],
        scratch_shapes=[
            pltpu.VMEM((rows, depth), bf16),
            pltpu.VMEM((depth, width), bf16),
            pltpu.VMEM((rows, width), f32),
            pltpu.SemaphoreType.DMA((chunks, 1 + len(weights))),
        ],
        compiler_params=params(16384),
        name="project",
    )(order, freqs, tokens, *weights)


def rope_kernel(turned, own_ref, recv_ref, cos_ref, sin_ref, out_ref):
    cosine = cos_ref[...]
    lane = lax.broadcasted_iota(jnp.int32, sin_ref.shape, 1)
    sine = jnp.where(lane < HD // 2, -sin_ref[...], sin_ref[...])
    for h in range(out_ref.shape[2] // HD):
        cols = slice(h * HD, (h + 1) * HD)
        x = own_ref[:, cols] + recv_ref[:, cols]
        if h < turned:
            x = x * cosine + pltpu.roll(x, HD // 2, 1) * sine
        for e in range(out_ref.shape[0]):
            out_ref[e, :, cols] = x.astype(bf16)


def rope(own, send, cosine, sine, turned, copies):
    recv = lax.ppermute(send, "row", [(0, 1), (1, 0)])
    return pl.pallas_call(
        partial(rope_kernel, turned),
        in_specs=[VMEM] * 4,
        out_specs=VMEM,
        out_shape=jax.ShapeDtypeStruct((copies, *own.shape), bf16),
        compiler_params=params(8192),
        name="rope",
    )(own, recv, cosine, sine)


def attend_kernel(order_ref, q_ref, own_ref, other_ref, ow_hbm, out_ref, ow_ref, sem):
    fetch = pltpu.make_async_copy(ow_hbm, ow_ref, sem)
    fetch.start()
    yh, z, row = place()
    peers_a, tok, width = q_ref.shape
    peers_e = own_ref.shape[0]
    part = tok // 2
    heads = width // HD
    rows = heads * part
    keys = peers_e * part

    lane = lax.broadcasted_iota(jnp.int32, (1, keys), 1)
    low_base = jnp.zeros((1, keys), jnp.int32)
    high_base = jnp.zeros((1, keys), jnp.int32)
    for e in range(peers_e):
        at = (lane >= e * part) & (lane < (e + 1) * part)
        slot = 2 * (yh * peers_e + e)
        low_base = jnp.where(at, order_ref[slot], low_base)
        high_base = jnp.where(at, order_ref[slot + 1], high_base)
    inner = lane & (part - 1)

    def side(base, core):
        return base * (2 * part) + inner + core * part

    low_pos = jnp.concatenate([side(low_base, row), side(low_base, 1 - row)], axis=1)
    high_pos = jnp.concatenate([side(high_base, row), side(high_base, 1 - row)], axis=1)

    def both(first, last, c0):
        pieces = [
            ref[:, first:last, c0 : c0 + HD].reshape(keys, HD) for ref in (own_ref, other_ref)
        ]
        return jnp.concatenate(pieces, axis=0)

    ones = jnp.where(lax.broadcasted_iota(jnp.int32, (2 * keys, HD), 1) == 0, 1.0, 0.0).astype(bf16)
    k_low, k_high = both(0, part, 0), both(part, tok, 0)
    v_low = jnp.concatenate([both(0, part, HD), ones], axis=1)
    v_high = jnp.concatenate([both(part, tok, HD), ones], axis=1)
    q_inner = lax.broadcasted_iota(jnp.int32, (rows, 1), 0) & (part - 1)
    spot = lax.broadcasted_iota(jnp.int32, (rows, HD), 1)

    for turn in range(peers_a):
        a = (yh + turn) & (peers_a - 1)
        slot = 2 * (a * peers_e + z)
        b_low, b_high = order_ref[slot], order_ref[slot + 1]
        mine = q_ref.at[a]

        def stacked(first, last):
            return [mine[first:last, h * HD : (h + 1) * HD] for h in range(heads)]

        q_both = jnp.concatenate(stacked(0, part) + stacked(part, tok), axis=0)
        s_low = dot_t(q_both, k_low)
        s_ll, s_hl = s_low[:rows], s_low[rows:]
        s_hh = dot_t(q_both[rows:], k_high)
        if turn == 0:
            s_ll = jnp.where(low_pos <= b_low * (2 * part) + row * part + q_inner, s_ll, large_negative)
            s_hh = jnp.where(high_pos <= b_high * (2 * part) + row * part + q_inner, s_hh, large_negative)
        else:
            s_ll = s_ll + jnp.where(low_pos < b_low * (2 * part), 0.0, large_negative)
            s_hh = s_hh + jnp.where(high_pos < b_high * (2 * part), 0.0, large_negative)
        m_low = jnp.maximum(jnp.max(s_ll, axis=1, keepdims=True), large_negative * 0.1)
        m_high = jnp.maximum(
            jnp.max(s_hl, axis=1, keepdims=True), jnp.max(s_hh, axis=1, keepdims=True)
        )
        p_ll = jnp.exp2((s_ll - m_low) * score_to_log2).astype(bf16)
        p_hl = jnp.exp2((s_hl - m_high) * score_to_log2).astype(bf16)
        p_hh = jnp.exp2((s_hh - m_high) * score_to_log2).astype(bf16)
        o_both = jnp.dot(jnp.concatenate([p_ll, p_hl], axis=0), v_low, preferred_element_type=f32)
        o_low = o_both[:rows]
        o_high = o_both[rows:] + jnp.dot(p_hh, v_high, preferred_element_type=f32)

        logs = jnp.zeros((rows, HD), f32)
        for i, (m, o) in enumerate(((m_low, o_low), (m_high, o_high))):
            d = o[:, HD : HD + 1]
            seen = d > 0.0
            safe = jnp.where(seen, d, 1.0)
            out_ref[a, i * rows : (i + 1) * rows, :] = (o[:, :HD] * (1.0 / safe)).astype(bf16)
            log = jnp.where(seen, m * score_to_log2 + jnp.log2(safe), large_negative)
            for j in range(3):
                piece = log.astype(bf16).astype(f32)
                logs = jnp.where(spot == 3 * i + j, piece, logs)
                log = log - piece
        out_ref[a, 2 * rows :, :] = logs.T[:16, :].astype(bf16)
    fetch.wait()


def attend(block_order, queries, own_keys, other_keys, output_weight):
    peers, tok, width = queries.shape
    return pl.pallas_call(
        attend_kernel,
        in_specs=[SMEM, VMEM, VMEM, VMEM, HBM],
        out_specs=[VMEM] * 2,
        out_shape=[
            jax.ShapeDtypeStruct((peers, tok * width // HD + 16, HD), bf16),
            jax.ShapeDtypeStruct(output_weight.shape, bf16),
        ],
        scratch_shapes=[pltpu.SemaphoreType.DMA],
        compiler_params=params(24576),
        name="attend",
    )(block_order, queries, own_keys, other_keys, output_weight)


def output_kernel(parts_ref, ow_ref, out_ref, att):
    peers, _, _ = parts_ref.shape
    tok, width = att.shape
    part = tok // 2
    heads = width // HD
    rows = heads * part

    shares = []
    for i in range(2):
        logs = []
        for p in range(peers):
            got = parts_ref[p, 2 * rows : 2 * rows + 16, :].astype(f32)
            logs.append(got[3 * i : 3 * i + 1] + got[3 * i + 1 : 3 * i + 2] + got[3 * i + 2 : 3 * i + 3])
        top = logs[0]
        for log in logs[1:]:
            top = jnp.maximum(top, log)
        weights = [jnp.exp2(log - top) for log in logs]
        total = weights[0]
        for w in weights[1:]:
            total = total + w
        shares += [w / total for w in weights]
    filled = jnp.concatenate(shares + [jnp.zeros((HD - 2 * peers, rows), f32)], axis=0)
    columns = filled.T
    for i in range(2):
        joined = jnp.zeros((rows, HD), f32)
        for p in range(peers):
            at = i * peers + p
            got = parts_ref[p, i * rows : (i + 1) * rows, :].astype(f32)
            joined += columns[:, at : at + 1] * got
        joined = joined.astype(bf16)
        for h in range(heads):
            att[i * part : (i + 1) * part, h * HD : (h + 1) * HD] = joined[h * part : (h + 1) * part, :]

    size = out_ref.shape[2]
    for k in range(out_ref.shape[0]):
        cols = slice(k * size, (k + 1) * size)
        out_ref[k] = jnp.dot(att[...], ow_ref[:, cols], preferred_element_type=f32).astype(bf16)


def output(parts, output_weight, tok, peers):
    width, columns = output_weight.shape
    return pl.pallas_call(
        output_kernel,
        in_specs=[VMEM] * 2,
        out_specs=VMEM,
        out_shape=jax.ShapeDtypeStruct((peers, tok, columns // peers), bf16),
        scratch_shapes=[pltpu.VMEM((tok, width), bf16)],
        compiler_params=params(12288),
        name="output",
    )(parts, output_weight)


def gather_kernel(recv_ref, out_ref):
    part = recv_ref.shape[1] // 2
    peers = recv_ref.shape[0] // 2
    for core in range(2):
        total = recv_ref[core * peers].astype(f32)
        for c in range(1, peers):
            total = total + recv_ref[core * peers + c].astype(f32)
        for k in range(2):
            at = 2 * k * part + core * part
            out_ref[at : at + part, :] = total[k * part : (k + 1) * part, :]


def body(tokens, block_order, query_weight, key_weight, value_weight, output_weight):
    rows_here = tokens.shape[0]
    tok = rows_here // 2
    q_width = query_weight.shape[1]

    half_width = HD // 2
    freqs = rope_theta ** (-(jnp.arange(half_width, dtype=f32) * 2.0 / HD))
    freqs = jnp.concatenate([freqs, freqs])[None]
    block_order, tokens, query_weight, key_weight, value_weight, output_weight = (
        pltpu.with_memory_space_constraint(array, pltpu.HBM)
        for array in (block_order, tokens, query_weight, key_weight, value_weight, output_weight)
    )
    own, send, angles = project(block_order, freqs, tokens, key_weight, value_weight)
    cosine, sine = jnp.cos(angles), jnp.sin(angles)
    key_values = rope(own, send, cosine, sine, 1, lax.axis_size("z"))
    own_keys = lax.all_to_all(key_values, "z", 0, 0)
    own, send, _ = project(block_order, freqs, tokens, query_weight)
    queries = rope(own, send, cosine, sine, q_width // HD, 1)[0]
    all_queries = lax.all_gather(queries, "yh")
    other_keys = lax.ppermute(own_keys, "row", [(0, 1), (1, 0)])

    result, fetched = attend(block_order, all_queries, own_keys, other_keys, output_weight)
    parts = lax.all_to_all(result, "yh", 0, 0)
    across = ("row", "x", "yl")
    partial_out = output(parts, fetched, tok, lax.axis_size(across))
    shares = lax.all_to_all(partial_out, across, 0, 0)
    return pl.pallas_call(
        gather_kernel,
        in_specs=[VMEM],
        out_specs=VMEM,
        out_shape=jax.ShapeDtypeStruct((rows_here, shares.shape[2]), f32),
        compiler_params=params(8192),
        name="gather",
    )(shares)


def solution(mesh):
    seq, row, col = (mesh.shape[name] for name in ("seq", "row", "col"))
    z = min(16, seq // 2)
    yl = 2 if col == 8 else 1
    devices = mesh.devices.reshape(seq // z, z, row, col // yl, yl)
    fine = Mesh(devices, ("yh", "z", "row", "x", "yl"))
    seq_axes, col_axes = ("yh", "z"), ("x", "yl")
    placed = (
        P(seq_axes, "row"),
        P(),
        P("row", col_axes),
        P("row", col_axes),
        P("row", col_axes),
        P(col_axes, None),
    )
    return jax.shard_map(
        body,
        mesh=fine,
        in_specs=placed,
        out_specs=P(seq_axes, ("row", *col_axes)),
        check_vma=False,
    )
```
